512 devices in a mesh: replica: 32 (over y, x), owner: 16 (over z, core).
Axes of the slice: x: 4, y: 8, z: 8, core: 2. Of those that a mesh axis runs over, the one named last changes fastest.
Arguments:
- owner_of: int32 [24], replicated, may hold values from 0 to 15, as said below
- grad: bfloat16 [32, 32, 2304, 128], P('replica', 'owner')
- error: bfloat16 [32, 32, 2304, 128], P('replica', 'owner'), may hold values from -4 to 4
- q_prev: float32 [32, 128, 32], P('owner')
- weight: float32 [32, 2304, 128], P('owner', 'replica'), may hold values from -0.125 to 0.125
- momentum: float32 [32, 2304, 128], P('owner', 'replica'), may hold values from -1.2 to 1.2
- vec_grad: bfloat16 [32, 128, 2304], P('replica', 'owner')
- vec_weight: float32 [128, 2304], P('owner', 'replica'), may hold values from 0.5 to 1.5
- vec_mom: float32 [128, 2304], P('owner', 'replica'), may hold values from -1.2 to 1.2
Outputs:
- weight_next: float32 [32, 2304, 128], P('owner', 'replica')
- momentum_next: float32 [32, 2304, 128], P('owner', 'replica')
- error_next: bfloat16 [32, 32, 2304, 128], P('replica', 'owner')
- q_next: float32 [32, 128, 32], P('owner')
- vec_weight_next: float32 [128, 2304], P('owner', 'replica')
- vec_mom_next: float32 [128, 2304], P('owner', 'replica')
The draws below stay inside these ranges and needn't reach their ends.
Inputs may be any that keep to these rules, and one draw needn't show every extreme that they name: `owner_of`: every owner index appears once or twice; half of them appear twice.
All inputs are finite; a program needn't handle non-finite values.
Results may differ from the reference program's by a relative error of at most 0.001.
Values sent between devices are 32-bit elements; how exact they have to be, the bound alone decides.
A program may use at most 64 MiB of HBM per device.

```python
import math
import jax
import jax.numpy as jnp
from jax import lax

D = 2304
WIN = 128
R = 32
SLOTS = 2
VEC_DEV = 8
NS_ITERS = 5
MATS = 24
SLOTS_ALL = 32
VECS = 128
N_REPLICA = 32
N_OWNER = 16


def rising(length, top):
    return top ** (jnp.arange(length, dtype=jnp.float32) / max(length - 1, 1))


def draw_owner_of(key, part):
    key_first, key_second = jax.random.split(key)
    extra = jax.random.permutation(key_first, jnp.arange(N_OWNER, dtype=jnp.int32))[:N_OWNER // 2]
    listing = jnp.concatenate([jnp.arange(N_OWNER, dtype=jnp.int32), extra])
    return jax.random.permutation(key_second, listing)


def draw_grad(key, part):
    key_rows, key_cols, key_noise = jax.random.split(key, 3)
    ramp_top = 3.0
    slot_total = N_OWNER * SLOTS
    owner_ramp = jnp.repeat(rising(N_OWNER, math.sqrt(ramp_top)), SLOTS)
    row_ramp = rising(D, math.sqrt(ramp_top))
    row_scale = jnp.exp(jax.random.uniform(key_rows, (slot_total, D, 1), jnp.float32, 0.0, math.log(3.0)))
    col_scale = jnp.exp(jax.random.uniform(key_cols, (slot_total, 1, WIN), jnp.float32, 0.0, math.log(3.0)))
    noise = jax.random.normal(key_noise, (N_REPLICA, slot_total, D, WIN), jnp.float32)
    shaped = row_scale * col_scale * owner_ramp[:, None, None] * row_ramp[None, :, None]
    return (noise * shaped[None]).astype(jnp.bfloat16)


def draw_q_prev(key, part):
    key_noise, key_common, key_cols = jax.random.split(key, 3)
    slot_total = N_OWNER * SLOTS
    noise = jax.random.normal(key_noise, (slot_total, WIN, R), jnp.float32)
    common = jax.random.normal(key_common, (slot_total, WIN, 1), jnp.float32)
    col_scale = jnp.exp(jax.random.uniform(key_cols, (slot_total, 1, R), jnp.float32, 0.0, math.log(3.0)))
    return (noise + 0.6 * common) * col_scale


def draw_vec_grad(key, part):
    key_noise = jax.random.fold_in(key, 0)
    key_rows = jax.random.fold_in(key, 2)
    ramp_top = 3.0
    vec_total = N_OWNER * VEC_DEV
    owner_ramp = jnp.repeat(rising(N_OWNER, math.sqrt(ramp_top)), VEC_DEV)
    col_ramp = rising(D, math.sqrt(ramp_top))
    row_scale = jnp.exp(jax.random.uniform(key_rows, (vec_total, 1), jnp.float32, 0.0, math.log(3.0)))
    noise = jax.random.normal(key_noise, (N_REPLICA, vec_total, D), jnp.float32)
    shaped = row_scale * owner_ramp[:, None] * col_ramp[None, :]
    return (noise * shaped[None]).astype(jnp.bfloat16)


def steps_of(stream_key, extent, shards, low, high):
    def one(axis_at, parts):
        heights = jax.random.uniform(jax.random.fold_in(jax.random.fold_in(stream_key, 6), axis_at), (parts,), jnp.float32, low / len(shards), high / len(shards))
        return jnp.repeat(jnp.exp(heights), extent[axis_at] // parts).reshape((-1,) + (1,) * (len(extent) - axis_at - 1))

    loudness = one(*shards[0])
    for cut in shards[1:]:
        loudness = loudness * one(*cut)
    return loudness


def gaussian(rng, extent, scale, reach, cuts=(), held_as=jnp.bfloat16):
    entries = jax.random.normal(rng, extent, jnp.float32) * scale
    if len(cuts) > 0:
        entries = steps_of(rng, extent, cuts, -0.22, 0.18) * entries
    return jnp.clip(entries, min=-reach, max=reach).astype(held_as)


def setup_inputs(seed: int = 0) -> dict:
    key_of = jax.random.split(jax.random.key(seed), 10)
    owner_of = draw_owner_of(jax.random.fold_in(key_of[9], 71), 0)
    grad = draw_grad(jax.random.fold_in(key_of[9], 71), 0)
    error = gaussian(key_of[2], (N_REPLICA, SLOTS_ALL, D, WIN), 0.5, 4.0, ((0, 32), (1, 16)))
    q_prev = draw_q_prev(jax.random.fold_in(key_of[9], 71), 0)
    weight = gaussian(key_of[4], (SLOTS_ALL, D, WIN), D ** -0.5, 0.125, ((0, 16), (1, 32)), jnp.float32)
    momentum = gaussian(key_of[5], (SLOTS_ALL, D, WIN), 0.2, 1.2, ((0, 16), (1, 32)), jnp.float32)
    vec_grad = draw_vec_grad(jax.random.fold_in(key_of[9], 71), 0)
    vec_weight = jnp.clip(1.0 + 0.1 * jax.random.normal(key_of[7], (VECS, D), jnp.float32), 0.5, 1.5)
    vec_mom = gaussian(key_of[8], (VECS, D), 0.2, 1.2, ((0, 16), (1, 32)), jnp.float32)
    return {"owner_of": owner_of, "grad": grad, "error": error, "q_prev": q_prev, "weight": weight, "momentum": momentum, "vec_grad": vec_grad, "vec_weight": vec_weight, "vec_mom": vec_mom}


exact_mode = lax.Precision.HIGHEST
clip_limit = 0.1
momentum_decay = 0.9
learn_rate = 0.05

def inverse_root(gram_mat, iterations):
    identity = jnp.eye(gram_mat.shape[-1], dtype=jnp.float32)
    scale_sq = jnp.sqrt(lax.optimization_barrier(jnp.sum(gram_mat * gram_mat, axis=(1, 2), keepdims=True)) + 1e-06)
    current = gram_mat / scale_sq
    inv_root = jnp.broadcast_to(identity, gram_mat.shape)
    for iteration in range(iterations):
        factor_mat = 1.5 * identity - 0.5 * jnp.einsum('sij,sjk->sik', inv_root, current, precision=exact_mode)
        current = jnp.einsum('sij,sjk->sik', current, factor_mat, precision=exact_mode)
        inv_root = jnp.einsum('sij,sjk->sik', factor_mat, inv_root, precision=exact_mode)
    return (inv_root, scale_sq)

def one_slot(inputs):
    grad_slot, error_slot, q_slot = inputs
    merged = grad_slot.astype(jnp.float32) + error_slot.astype(jnp.float32)
    p_sum = jnp.einsum('rdw,wk->dk', merged, q_slot, precision=exact_mode)
    gram_mat = jnp.dot(p_sum.T, p_sum, precision=exact_mode)
    inv_root, scale_sq = inverse_root(gram_mat[None], NS_ITERS)
    p_hat = jnp.dot(p_sum, inv_root[0], precision=exact_mode) / jnp.sqrt(scale_sq[0])
    q_new = jnp.einsum('rdw,dk->wk', merged, p_hat, precision=exact_mode) / N_REPLICA
    approx = jnp.dot(p_hat, q_new.T, precision=exact_mode)
    error_new = (merged - approx[None]).astype(jnp.bfloat16)
    return (approx, error_new, q_new)

def reference(owner_of, grad, error, q_prev, weight, momentum, vec_grad, vec_weight, vec_mom):
    owner_ids = jnp.arange(N_OWNER, dtype=jnp.int32)
    counts = lax.optimization_barrier(jnp.sum((owner_of[None, :] == owner_ids[:, None]).astype(jnp.int32), axis=1))
    live_slots = (jnp.arange(SLOTS, dtype=jnp.int32)[None, :] < counts[:, None]).reshape(-1)
    approx, error_new, q_new = lax.map(one_slot, (jnp.moveaxis(grad, 1, 0), jnp.moveaxis(error, 1, 0), q_prev))
    error_new = jnp.moveaxis(error_new, 0, 1)
    live_mask = live_slots[:, None, None]
    vec_mean = lax.optimization_barrier(jnp.sum(vec_grad.astype(jnp.float32), axis=0)) / N_REPLICA
    total_sq = jnp.sum(jnp.where(live_mask, approx * approx, 0.0)) + jnp.sum(vec_mean * vec_mean)
    entry_count = float(MATS * D * WIN + VECS * D)
    factor = jnp.minimum(1.0, clip_limit / jnp.sqrt(total_sq / entry_count + 1e-06))
    momentum_next = jnp.where(live_mask, momentum_decay * momentum + factor * approx, momentum)
    weight_next = jnp.where(live_mask, weight - learn_rate * momentum_next, weight)
    error_next = jnp.where(live_slots[None, :, None, None], error_new, error)
    q_next = jnp.where(live_mask, q_new, q_prev)
    vec_mom_next = momentum_decay * vec_mom + factor * vec_mean
    vec_weight_next = vec_weight - learn_rate * vec_mom_next
    return (weight_next, momentum_next, error_next, q_next, vec_weight_next, vec_mom_next)
```

```python
import functools

import jax
import jax.numpy as jnp
from jax import lax
from jax.experimental import pallas as pl
from jax.experimental.pallas import tpu as pltpu
from jax.sharding import PartitionSpec as P

MESH = pl.DeviceIdType.MESH
NS_ITERS = 5
NX, NY, NO = 4, 8, 16
clip_limit = 0.1
momentum_decay = 0.9
learn_rate = 0.05
f32, bf16 = jnp.float32, jnp.bfloat16
HIGH = lax.Precision.HIGHEST


def split(a):
    hi = a.astype(bf16)
    return hi, (a - hi.astype(f32)).astype(bf16)


def dot(a, b, dims=((1,), (0,)), precision=None):
    return lax.dot_general(a, b, (dims, ((), ())), precision=precision, preferred_element_type=f32)


def gather_kernel(
    own_ref, grad_ref, err_ref, q_ref, vec_ref,
    pf_ref, b_ref, qt_ref, vs_ref, fac_ref,
    gv, ev, qv, vv, loc, rx0, c0, ry0, own0, gy0, ry1, c1, rx1, own1, gx1,
    vpk, vrx, vc, vry, tt, try_, tx, tf, sc,
    load_sem, send_sem, recv_sem,
    *, entries,
):
    r = lax.axis_index("replica")
    o = lax.axis_index("owner")
    x, y = lax.rem(r, NX), r // NX

    def xpeer(d):
        return (y * NX + lax.rem(x + d, NX), o)

    def ypeer(d):
        return (lax.rem(y + d, NY) * NX + x, o)

    def opeer(d):
        return (r, lax.rem(o + d, NO))

    barrier = pltpu.get_barrier_semaphore()
    peers = [xpeer(d) for d in range(1, NX)] + [ypeer(d) for d in range(1, NY)] + [opeer(d) for d in range(1, NO)]
    for peer in peers:
        pl.semaphore_signal(barrier, inc=1, device_id=peer, device_id_type=MESH)

    loads = []
    for n, (src, dst) in enumerate(
        [(q_ref, qv), (grad_ref.at[0, 0], gv.at[0]), (err_ref.at[0, 0], ev.at[0]),
         (grad_ref.at[0, 1], gv.at[1]), (err_ref.at[0, 1], ev.at[1]), (vec_ref.at[0], vv)]
    ):
        copy = pltpu.make_async_copy(src, dst, load_sem.at[n])
        copy.start()
        loads.append(copy)

    started = []

    def send(src, dst, peer):
        n = len(started)
        copy = pltpu.make_async_remote_copy(
            src_ref=src, dst_ref=dst, send_sem=send_sem.at[n], recv_sem=recv_sem.at[n],
            device_id=peer, device_id_type=MESH,
        )
        copy.start()
        started.append(copy)
        return copy

    def arrive(copies):
        for copy in copies:
            copy.wait_recv()

    lane_block = lax.broadcasted_iota(jnp.int32, (128, 128), 1) // 32
    row_block = lax.broadcasted_iota(jnp.int32, (128, 128), 0) // 32
    lane_k = lax.broadcasted_iota(jnp.int32, (128, 128), 1)
    row_k = lax.broadcasted_iota(jnp.int32, (128, 128), 0)

    def left(s):
        wide = jnp.concatenate([qv[s]] * 4, axis=1)
        hi, lo = split(wide)
        total = None
        for j in range(4):
            keep = lane_block == j
            zero = jnp.zeros_like(hi)
            half = jnp.concatenate([jnp.where(keep, hi, zero), jnp.where(keep, lo, zero)], axis=1)
            rhs = jnp.concatenate([half, half], axis=0)
            rows = slice(576 * j, 576 * j + 576)
            term = dot(jnp.concatenate([gv[s, rows], ev[s, rows]], axis=1), rhs)
            total = term if total is None else total + term
        loc[s] = total[:, :128] + total[:, 128:]

    loads[0].wait()
    loads[1].wait()
    loads[2].wait()
    left(0)
    pl.semaphore_wait(barrier, len(peers))

    x0 = []
    for d in (2, 1, 3):
        to = lax.rem(x + d, NX)
        x0.append(send(loc.at[0, pl.ds(pl.multiple_of(to * 144, 8), 144)], rx0.at[d - 1], xpeer(d)))
    loads[3].wait()
    loads[4].wait()
    left(1)
    y1 = []
    for d in (4, 3, 5, 2, 6, 1, 7):
        to = lax.rem(y + d, NY)
        y1.append(send(loc.at[1, pl.ds(pl.multiple_of(to * 72, 8), 72)], ry1.at[d - 1], ypeer(d)))

    loads[5].wait()
    vall = vv[...].astype(f32)
    for yy in range(NY):
        for xx in range(NX):
            at = 72 * (NX * yy + xx)
            piece = jnp.concatenate([vall[:, at:at + 72], jnp.zeros((8, 56), f32)], axis=1)
            vpk[xx * NY + yy] = piece

    arrive(x0)
    acc = loc[0, pl.ds(pl.multiple_of(x * 144, 8), 144)] + rx0[0] + rx0[1] + rx0[2]
    pad = jnp.zeros((6, 128), f32)
    for yy in range(NY):
        c0[yy] = jnp.concatenate([acc[18 * yy:18 * yy + 18], pad], axis=0)
    y0 = []
    for d in (4, 3, 5, 2, 6, 1, 7):
        y0.append(send(c0.at[lax.rem(y + d, NY)], ry0.at[d - 1], ypeer(d)))

    arrive(y1)
    acc = loc[1, pl.ds(pl.multiple_of(y * 72, 8), 72)]
    for d in range(7):
        acc = acc + ry1[d]
    for xx in range(NX):
        c1[xx] = jnp.concatenate([acc[18 * xx:18 * xx + 18], pad], axis=0)
    x1 = []
    for d in (2, 1, 3):
        x1.append(send(c1.at[lax.rem(x + d, NX)], rx1.at[d - 1], xpeer(d)))

    vx = []
    for d in (2, 1, 3):
        to = lax.rem(x + d, NX)
        vx.append(send(vpk.at[pl.ds(to * NY, NY)], vrx.at[d - 1], xpeer(d)))

    arrive(y0)
    acc = c0[y]
    for d in range(7):
        acc = acc + ry0[d]
    own0[...] = acc
    gy0[y] = acc
    g0 = [send(own0, gy0.at[y], ypeer(d)) for d in (4, 3, 5, 2, 6, 1, 7)]

    arrive(x1)
    acc = c1[x] + rx1[0] + rx1[1] + rx1[2]
    own1[...] = acc
    gx1[x] = acc
    g1 = [send(own1, gx1.at[x], xpeer(d)) for d in (2, 1, 3)]

    arrive(g0)
    mine0 = pl.ds(pl.multiple_of(x * 144, 8), 144)
    pf_ref[0, mine0] = jnp.concatenate([gy0[yy, 0:18] for yy in range(NY)], axis=0)
    h0 = [send(pf_ref.at[0, mine0], pf_ref.at[0, mine0], xpeer(d)) for d in (2, 1, 3)]

    arrive(g1)
    mine1 = pl.ds(pl.multiple_of(y * 72, 8), 72)
    pf_ref[1, mine1] = jnp.concatenate([gx1[xx, 0:18] for xx in range(NX)], axis=0)
    h1 = [send(pf_ref.at[1, mine1], pf_ref.at[1, mine1], ypeer(d)) for d in (4, 3, 5, 2, 6, 1, 7)]

    arrive(vx)
    vc[...] = vpk[pl.ds(x * NY, NY)] + vrx[0] + vrx[1] + vrx[2]
    vy = []
    for d in (4, 3, 5, 2, 6, 1, 7):
        vy.append(send(vc.at[lax.rem(y + d, NY)], vry.at[d - 1], ypeer(d)))

    def right(s):
        hi, lo = split(pf_ref[s])
        lhs = jnp.concatenate([hi, lo], axis=1)
        total = None
        for j in range(4):
            rows = slice(576 * j, 576 * j + 576)
            term = dot(lhs, jnp.concatenate([gv[s, rows], ev[s, rows]], axis=1), ((0,), (0,)))
            term = term[32 * j:32 * j + 32] + term[128 + 32 * j:160 + 32 * j]
            total = term if total is None else total + term
        total = total[:, :128] + total[:, 128:]
        for i in range(4):
            tt[4 * s + i] = total[8 * i:8 * i + 8]

    arrive(h0)
    right(0)
    arrive(h1)
    right(1)
    ty = []
    for d in (4, 3, 5, 2, 6, 1, 7):
        ty.append(send(tt.at[lax.rem(y + d, NY)], try_.at[d - 1], ypeer(d)))

    gram = None
    for s in range(2):
        p = pf_ref[s]
        wide = jnp.where(row_block == lane_block, dot(p, p, ((0,), (0,)), HIGH), 0.0)
        pick = (lane_k == 32 * s + lax.rem(row_k, 32)).astype(f32)
        term = dot(pick, dot(wide, pick, precision=HIGH), ((0,), (0,)), HIGH)
        gram = term if gram is None else gram + term
    squares = gram * gram
    slot_of = row_k[:, :1] // 32
    sums = jnp.sum(squares, axis=1, keepdims=True)
    scale = [jnp.sqrt(jnp.sum(jnp.where(slot_of == s, sums, 0.0), axis=0, keepdims=True) + 1e-06) for s in range(2)]
    scale_row = jnp.where(slot_of == 0, scale[0], scale[1])
    eye = (row_k == lane_k).astype(f32)
    cur = gram / scale_row
    root = eye
    for step in range(NS_ITERS):
        fm = 1.5 * eye - 0.5 * (cur if step == 0 else dot(root, cur, precision=HIGH))
        if step < NS_ITERS - 1:
            cur = dot(cur, fm, precision=HIGH)
        root = fm if step == 0 else dot(fm, root, precision=HIGH)
    inv_sqrt = 1.0 / jnp.sqrt(scale_row)
    pm = dot(root, dot(gram, root, precision=HIGH), ((0,), (0,)), HIGH) / scale_row

    arrive(vy)
    vsum = vc[y]
    for d in range(7):
        vsum = vsum + vry[d]
    vs_ref[...] = vsum
    vmean = vsum * (1.0 / 32.0)
    vsq = jnp.sum(jnp.sum(vmean * vmean, axis=1, keepdims=True), axis=0, keepdims=True)

    arrive(ty)
    acc = tt[y]
    for d in range(7):
        acc = acc + try_[d]
    tx[x] = jnp.concatenate([acc, jnp.broadcast_to(vsq, (8, 128))], axis=0)
    t2 = [send(tx.at[x], tx.at[x], xpeer(d)) for d in (2, 1, 3)]
    arrive(t2)
    tf[y] = (tx[0] + tx[1]) + (tx[2] + tx[3])
    t3 = [send(tf.at[y], tf.at[y], ypeer(d)) for d in (4, 3, 5, 2, 6, 1, 7)]
    arrive(t3)
    tfull = jnp.concatenate([tf[yy, 0:8] for yy in range(NY)] + [jnp.zeros((64, 128), f32)], axis=0)
    vtot = tf[0, 8:16]
    for yy in range(1, NY):
        vtot = vtot + tf[yy, 8:16]

    count = jnp.int32(0)
    for n in range(own_ref.shape[0]):
        count = count + jnp.where(own_ref[n] == o, 1, 0).astype(jnp.int32)
    live_row = (slot_of < jnp.minimum(count, 2)).astype(f32)

    qt = dot(root, tfull, ((0,), (0,)), HIGH) * (inv_sqrt * (1.0 / 32.0))
    qm = dot(qt, qt, ((1,), (1,)), HIGH)
    part = jnp.sum(jnp.sum(pm * qm, axis=1, keepdims=True) * live_row, axis=0, keepdims=True)
    sc[o] = jnp.broadcast_to(part, (8, 128)) + vtot
    s1 = [send(sc.at[o], sc.at[o], opeer(d)) for d in (8, 7, 9, 6, 10, 5, 11, 4, 12, 3, 13, 2, 14, 1, 15)]
    b_ref[...] = (dot(root, qt, precision=HIGH) * inv_sqrt)[:64]
    qt_ref[...] = qt[:64]
    arrive(s1)
    total_sq = sc[0]
    for n in range(1, NO):
        total_sq = total_sq + sc[n]
    fac_ref[...] = jnp.minimum(1.0, clip_limit / jnp.sqrt(total_sq / entries + 1e-06))
    for copy in started:
        copy.wait_send()


def update_kernel(
    own_ref, fac_ref, pf_ref, b_ref, qt_ref, vs_ref, grad_ref, err_ref, q_ref, w_ref, m_ref, vw_ref, vm_ref,
    wn_ref, mn_ref, en_ref, qn_ref, vwn_ref, vmn_ref,
):
    r = lax.axis_index("replica")
    o = lax.axis_index("owner")
    s = pl.program_id(0)
    count = jnp.int32(0)
    for n in range(own_ref.shape[0]):
        count = count + jnp.where(own_ref[n] == o, 1, 0).astype(jnp.int32)
    live = s < count
    lane_block = lax.broadcasted_iota(jnp.int32, (128, 128), 0) // 32
    b = b_ref[...]
    wide = jnp.concatenate([b] * 4, axis=0)
    hi, lo = split(wide)
    zero = jnp.zeros_like(hi)
    phi, plo = split(pf_ref[...])
    lhs = jnp.concatenate([phi, plo], axis=1)

    def product(lhs, keep):
        bh, bl = jnp.where(keep, hi, zero), jnp.where(keep, lo, zero)
        return dot(lhs, jnp.concatenate([bh, bh], axis=0)) + dot(lhs[:, :128], bl)

    for j in range(4):
        rows = slice(576 * j, 576 * j + 576)
        approx = product(lhs, lane_block == j)
        e = err_ref[0, 0, rows]
        merged = grad_ref[0, 0, rows].astype(f32) + e.astype(f32)
        en_ref[0, 0, rows] = jnp.where(live, (merged - approx).astype(bf16), e)

    fac = fac_ref[0:1, :]
    at = pl.multiple_of(lax.rem(r, 8) * 72, 8)
    rhi, rlo = split(pf_ref[pl.ds(at, 72)])
    rows_lhs = jnp.concatenate([rhi, rlo], axis=1)
    approx = product(rows_lhs, lane_block == r // 8)
    m = m_ref[0]
    mn = jnp.where(live, momentum_decay * m + fac * approx, m)
    mn_ref[0] = mn
    w = w_ref[0]
    wn_ref[0] = jnp.where(live, w - learn_rate * mn, w)
    qn_ref[0] = jnp.where(live, qt_ref[...].T, q_ref[0])
    vmean = vs_ref[:, :72] * (1.0 / 32.0)
    vmn = momentum_decay * vm_ref[...] + fac[:, :72] * vmean
    vmn_ref[...] = vmn
    vwn_ref[...] = vw_ref[...] - learn_rate * vmn


def on_device(owner_of, grad, error, q_prev, weight, momentum, vec_grad, vec_weight, vec_mom):
    S = jax.ShapeDtypeStruct
    vm = pl.BlockSpec(memory_space=pltpu.VMEM)
    hbm = pl.BlockSpec(memory_space=pl.ANY)
    smem = pl.BlockSpec(memory_space=pltpu.SMEM)
    width = grad.shape[2]
    entries = float(owner_of.shape[0] * width * grad.shape[3] + NO * vec_grad.shape[1] * width)
    n_sends = 3 + 7 + 7 + 3 + 3 + 7 + 3 + 3 + 7 + 7 + 7 + 3 + 7 + 15
    V = pltpu.VMEM
    pf, b, qt, vs, fac = pl.pallas_call(
        functools.partial(gather_kernel, entries=entries),
        out_shape=(S((2, 576, 128), f32), S((64, 128), f32), S((64, 128), f32), S((8, 128), f32), S((8, 128), f32)),
        in_specs=[smem, hbm, hbm, hbm, hbm],
        out_specs=(vm, vm, vm, vm, vm),
        scratch_shapes=[
            V((2, 2304, 128), bf16), V((2, 2304, 128), bf16), V((2, 128, 32), f32), V((8, 2304), bf16),
            V((2, 576, 128), f32),
            V((3, 144, 128), f32), V((8, 24, 128), f32), V((7, 24, 128), f32), V((24, 128), f32), V((8, 24, 128), f32),
            V((7, 72, 128), f32), V((4, 24, 128), f32), V((3, 24, 128), f32), V((24, 128), f32), V((4, 24, 128), f32),
            V((32, 8, 128), f32), V((3, 8, 8, 128), f32), V((8, 8, 128), f32), V((7, 8, 128), f32),
            V((8, 8, 128), f32), V((7, 8, 128), f32), V((4, 16, 128), f32), V((8, 16, 128), f32), V((16, 8, 128), f32),
            pltpu.SemaphoreType.DMA((6,)),
            pltpu.SemaphoreType.DMA((n_sends,)),
            pltpu.SemaphoreType.DMA((n_sends,)),
        ],
        compiler_params=pltpu.CompilerParams(collective_id=0, has_side_effects=True),
        name="gather",
    )(owner_of, grad, error, q_prev, vec_grad)

    full = lambda shape: pl.BlockSpec(shape, lambda s: (0,) * len(shape))
    slot = lambda shape: pl.BlockSpec((1,) + shape, lambda s: (s,) + (0,) * len(shape))
    big = pl.BlockSpec((1, 1, 2304, 128), lambda s: (0, s, 0, 0))
    half = pl.BlockSpec((32, 128), lambda s: (s, 0))
    return pl.pallas_call(
        update_kernel,
        grid=(2,),
        out_shape=(
            S(weight.shape, f32), S(momentum.shape, f32), S(error.shape, bf16), S(q_prev.shape, f32),
            S(vec_weight.shape, f32), S(vec_mom.shape, f32),
        ),
        in_specs=[
            smem, full((8, 128)), pl.BlockSpec((None, 576, 128), lambda s: (s, 0, 0)), half, half, full((8, 128)),
            big, big, slot((128, 32)), slot((72, 128)), slot((72, 128)), full((8, 72)), full((8, 72)),
        ],
        out_specs=(
            slot((72, 128)), slot((72, 128)), big, slot((128, 32)), full((8, 72)), full((8, 72)),
        ),
        name="update",
    )(owner_of, fac, pf, b, qt, vs, grad, error, q_prev, weight, momentum, vec_weight, vec_mom)


def solution(mesh):
    return jax.shard_map(
        on_device,
        mesh=mesh,
        in_specs=(
            P(),
            P("replica", "owner", None, None),
            P("replica", "owner", None, None),
            P("owner", None, None),
            P("owner", "replica", None),
            P("owner", "replica", None),
            P("replica", "owner", None),
            P("owner", "replica"),
            P("owner", "replica"),
        ),
        out_specs=(
            P("owner", "replica", None),
            P("owner", "replica", None),
            P("replica", "owner", None, None),
            P("owner", None, None),
            P("owner", "replica"),
            P("owner", "replica"),
        ),
        check_vma=False,
    )
```

```python
import functools

import jax
import jax.numpy as jnp
from jax import lax
from jax.experimental import pallas as pl
from jax.experimental.pallas import tpu as pltpu
from jax.sharding import PartitionSpec as P

MESH = pl.DeviceIdType.MESH
NS_ITERS = 5
NX, NY, NO = 4, 8, 16
clip_limit = 0.1
momentum_decay = 0.9
learn_rate = 0.05
f32, bf16 = jnp.float32, jnp.bfloat16
HIGH = lax.Precision.HIGHEST


def split(a):
    hi = a.astype(bf16)
    return hi, (a - hi.astype(f32)).astype(bf16)


def dot(a, b, dims=((1,), (0,)), precision=None):
    return lax.dot_general(a, b, (dims, ((), ())), precision=precision, preferred_element_type=f32)


def gather_kernel(
    own_ref, grad_ref, err_ref, q_ref, vec_ref,
    pf_ref, b_ref, qt_ref, vs_ref, fac_ref,
    gv, ev, qv, vv, loc, rx0, c0, ry0, own0, gy0, ry1, c1, rx1, own1, gx1,
    vpk, vrx, vc, vry, tt, try_, tx, tf, sc,
    load_sem, send_sem, recv_sem,
    *, entries,
):
    r = lax.axis_index("replica")
    o = lax.axis_index("owner")
    x, y = lax.rem(r, NX), r // NX

    def xpeer(d):
        return (y * NX + lax.rem(x + d, NX), o)

    def ypeer(d):
        return (lax.rem(y + d, NY) * NX + x, o)

    def opeer(d):
        return (r, lax.rem(o + d, NO))

    barrier = pltpu.get_barrier_semaphore()
    peers = [xpeer(d) for d in range(1, NX)] + [ypeer(d) for d in range(1, NY)] + [opeer(d) for d in range(1, NO)]
    for peer in peers:
        pl.semaphore_signal(barrier, inc=1, device_id=peer, device_id_type=MESH)

    loads = []
    for n, (src, dst) in enumerate(
        [(q_ref, qv), (grad_ref.at[0, 0], gv.at[0]), (err_ref.at[0, 0], ev.at[0]),
         (grad_ref.at[0, 1], gv.at[1]), (err_ref.at[0, 1], ev.at[1]), (vec_ref.at[0], vv)]
    ):
        copy = pltpu.make_async_copy(src, dst, load_sem.at[n])
        copy.start()
        loads.append(copy)

    started = []

    def send(src, dst, peer):
        n = len(started)
        copy = pltpu.make_async_remote_copy(
            src_ref=src, dst_ref=dst, send_sem=send_sem.at[n], recv_sem=recv_sem.at[n],
            device_id=peer, device_id_type=MESH,
        )
        copy.start()
        started.append(copy)
        return copy

    def arrive(copies):
        for copy in copies:
            copy.wait_recv()

    lane_block = lax.broadcasted_iota(jnp.int32, (128, 128), 1) // 32
    row_block = lax.broadcasted_iota(jnp.int32, (128, 128), 0) // 32
    lane_k = lax.broadcasted_iota(jnp.int32, (128, 128), 1)
    row_k = lax.broadcasted_iota(jnp.int32, (128, 128), 0)

    def left(s):
        wide = jnp.concatenate([qv[s]] * 4, axis=0).T
        hi, lo = split(wide)
        total = None
        for j in range(4):
            keep = lane_block == j
            zero = jnp.zeros_like(hi)
            half = jnp.concatenate([jnp.where(keep, hi, zero), jnp.where(keep, lo, zero)], axis=1)
            rhs = jnp.concatenate([half, half], axis=0)
            rows = slice(576 * j, 576 * j + 576)
            term = dot(jnp.concatenate([gv[s, rows], ev[s, rows]], axis=1), rhs)
            total = term if total is None else total + term
        loc[s] = total[:, :128] + total[:, 128:]

    loads[0].wait()
    loads[1].wait()
    loads[2].wait()
    left(0)
    pl.semaphore_wait(barrier, len(peers))

    x0 = []
    for d in (2, 1, 3):
        to = lax.rem(x + d, NX)
        x0.append(send(loc.at[0, pl.ds(pl.multiple_of(to * 144, 8), 144)], rx0.at[d - 1], xpeer(d)))
    loads[3].wait()
    loads[4].wait()
    left(1)
    y1 = []
    for d in (4, 3, 5, 2, 6, 1, 7):
        to = lax.rem(y + d, NY)
        y1.append(send(loc.at[1, pl.ds(pl.multiple_of(to * 72, 8), 72)], ry1.at[d - 1], ypeer(d)))

    loads[5].wait()
    vall = vv[...].astype(f32)
    for yy in range(NY):
        for xx in range(NX):
            at = 72 * (NX * yy + xx)
            piece = jnp.concatenate([vall[:, at:at + 72], jnp.zeros((8, 56), f32)], axis=1)
            vpk[xx * NY + yy] = piece

    arrive(x0)
    acc = loc[0, pl.ds(pl.multiple_of(x * 144, 8), 144)] + rx0[0] + rx0[1] + rx0[2]
    pad = jnp.zeros((6, 128), f32)
    for yy in range(NY):
        c0[yy] = jnp.concatenate([acc[18 * yy:18 * yy + 18], pad], axis=0)
    y0 = []
    for d in (4, 3, 5, 2, 6, 1, 7):
        y0.append(send(c0.at[lax.rem(y + d, NY)], ry0.at[d - 1], ypeer(d)))

    arrive(y1)
    acc = loc[1, pl.ds(pl.multiple_of(y * 72, 8), 72)]
    for d in range(7):
        acc = acc + ry1[d]
    for xx in range(NX):
        c1[xx] = jnp.concatenate([acc[18 * xx:18 * xx + 18], pad], axis=0)
    x1 = []
    for d in (2, 1, 3):
        x1.append(send(c1.at[lax.rem(x + d, NX)], rx1.at[d - 1], xpeer(d)))

    vx = []
    for d in (2, 1, 3):
        to = lax.rem(x + d, NX)
        vx.append(send(vpk.at[pl.ds(to * NY, NY)], vrx.at[d - 1], xpeer(d)))

    arrive(y0)
    acc = c0[y]
    for d in range(7):
        acc = acc + ry0[d]
    own0[...] = acc
    gy0[y] = acc
    g0 = [send(own0, gy0.at[y], ypeer(d)) for d in (4, 3, 5, 2, 6, 1, 7)]

    arrive(x1)
    acc = c1[x] + rx1[0] + rx1[1] + rx1[2]
    own1[...] = acc
    gx1[x] = acc
    g1 = [send(own1, gx1.at[x], xpeer(d)) for d in (2, 1, 3)]

    arrive(g0)
    mine0 = pl.ds(pl.multiple_of(x * 144, 8), 144)
    pf_ref[0, mine0] = jnp.concatenate([gy0[yy, 0:18] for yy in range(NY)], axis=0)
    h0 = [send(pf_ref.at[0, mine0], pf_ref.at[0, mine0], xpeer(d)) for d in (2, 1, 3)]

    arrive(g1)
    mine1 = pl.ds(pl.multiple_of(y * 72, 8), 72)
    pf_ref[1, mine1] = jnp.concatenate([gx1[xx, 0:18] for xx in range(NX)], axis=0)
    h1 = [send(pf_ref.at[1, mine1], pf_ref.at[1, mine1], ypeer(d)) for d in (4, 3, 5, 2, 6, 1, 7)]

    arrive(vx)
    vc[...] = vpk[pl.ds(x * NY, NY)] + vrx[0] + vrx[1] + vrx[2]
    vy = []
    for d in (4, 3, 5, 2, 6, 1, 7):
        vy.append(send(vc.at[lax.rem(y + d, NY)], vry.at[d - 1], ypeer(d)))

    def right(s):
        hi, lo = split(pf_ref[s])
        lhs = jnp.concatenate([hi, lo], axis=1)
        total = None
        for j in range(4):
            rows = slice(576 * j, 576 * j + 576)
            term = dot(lhs, jnp.concatenate([gv[s, rows], ev[s, rows]], axis=1), ((0,), (0,)))
            term = term[32 * j:32 * j + 32] + term[128 + 32 * j:160 + 32 * j]
            total = term if total is None else total + term
        total = total[:, :128] + total[:, 128:]
        for i in range(4):
            tt[4 * s + i] = total[8 * i:8 * i + 8]

    arrive(h0)
    right(0)
    arrive(h1)
    right(1)
    ty = []
    for d in (4, 3, 5, 2, 6, 1, 7):
        ty.append(send(tt.at[lax.rem(y + d, NY)], try_.at[d - 1], ypeer(d)))

    gram = None
    for s in range(2):
        p = pf_ref[s]
        wide = jnp.where(row_block == lane_block, dot(p, p, ((0,), (0,)), HIGH), 0.0)
        pick = (lane_k == 32 * s + lax.rem(row_k, 32)).astype(f32)
        term = dot(pick, dot(wide, pick, precision=HIGH), ((0,), (0,)), HIGH)
        gram = term if gram is None else gram + term
    squares = gram * gram
    slot_of = row_k[:, :1] // 32
    sums = jnp.sum(squares, axis=1, keepdims=True)
    scale = [jnp.sqrt(jnp.sum(jnp.where(slot_of == s, sums, 0.0), axis=0, keepdims=True) + 1e-06) for s in range(2)]
    scale_row = jnp.where(slot_of == 0, scale[0], scale[1])
    eye = (row_k == lane_k).astype(f32)
    cur = gram / scale_row
    root = eye
    for step in range(NS_ITERS):
        fm = 1.5 * eye - 0.5 * (cur if step == 0 else dot(root, cur, precision=HIGH))
        if step < NS_ITERS - 1:
            cur = dot(cur, fm, precision=HIGH)
        root = fm if step == 0 else dot(fm, root, precision=HIGH)
    inv_sqrt = 1.0 / jnp.sqrt(scale_row)
    pm = dot(root, dot(gram, root, precision=HIGH), ((0,), (0,)), HIGH) / scale_row

    arrive(vy)
    vsum = vc[y]
    for d in range(7):
        vsum = vsum + vry[d]
    vs_ref[...] = vsum
    vmean = vsum * (1.0 / 32.0)
    vsq = jnp.sum(jnp.sum(vmean * vmean, axis=1, keepdims=True), axis=0, keepdims=True)

    arrive(ty)
    acc = tt[y]
    for d in range(7):
        acc = acc + try_[d]
    tx[x] = jnp.concatenate([acc, jnp.broadcast_to(vsq, (8, 128))], axis=0)
    t2 = [send(tx.at[x], tx.at[x], xpeer(d)) for d in (2, 1, 3)]
    arrive(t2)
    tf[y] = (tx[0] + tx[1]) + (tx[2] + tx[3])
    t3 = [send(tf.at[y], tf.at[y], ypeer(d)) for d in (4, 3, 5, 2, 6, 1, 7)]
    arrive(t3)
    tfull = jnp.concatenate([tf[yy, 0:8] for yy in range(NY)] + [jnp.zeros((64, 128), f32)], axis=0)
    vtot = tf[0, 8:16]
    for yy in range(1, NY):
        vtot = vtot + tf[yy, 8:16]

    count = jnp.int32(0)
    for n in range(own_ref.shape[0]):
        count = count + jnp.where(own_ref[n] == o, 1, 0).astype(jnp.int32)
    live_row = (slot_of < jnp.minimum(count, 2)).astype(f32)

    qt = dot(root, tfull, ((0,), (0,)), HIGH) * (inv_sqrt * (1.0 / 32.0))
    qm = dot(qt, qt, ((1,), (1,)), HIGH)
    part = jnp.sum(jnp.sum(pm * qm, axis=1, keepdims=True) * live_row, axis=0, keepdims=True)
    sc[o] = jnp.broadcast_to(part, (8, 128)) + vtot
    s1 = [send(sc.at[o], sc.at[o], opeer(d)) for d in (8, 7, 9, 6, 10, 5, 11, 4, 12, 3, 13, 2, 14, 1, 15)]
    b_ref[...] = (dot(root, qt, precision=HIGH) * inv_sqrt)[:64]
    qt_ref[...] = qt[:64]
    arrive(s1)
    total_sq = sc[0]
    for n in range(1, NO):
        total_sq = total_sq + sc[n]
    fac_ref[...] = jnp.minimum(1.0, clip_limit / jnp.sqrt(total_sq / entries + 1e-06))
    for copy in started:
        copy.wait_send()


def update_kernel(
    own_ref, fac_ref, pf_ref, b_ref, qt_ref, vs_ref, grad_ref, err_ref, q_ref, w_ref, m_ref, vw_ref, vm_ref,
    wn_ref, mn_ref, en_ref, qn_ref, vwn_ref, vmn_ref,
):
    r = lax.axis_index("replica")
    o = lax.axis_index("owner")
    s = pl.program_id(0)
    count = jnp.int32(0)
    for n in range(own_ref.shape[0]):
        count = count + jnp.where(own_ref[n] == o, 1, 0).astype(jnp.int32)
    live = s < count
    lane_block = lax.broadcasted_iota(jnp.int32, (128, 128), 0) // 32
    b = b_ref[...]
    wide = jnp.concatenate([b] * 4, axis=0)
    hi, lo = split(wide)
    zero = jnp.zeros_like(hi)
    phi, plo = split(pf_ref[...])
    lhs = jnp.concatenate([phi, plo], axis=1)

    def product(lhs, keep):
        bh, bl = jnp.where(keep, hi, zero), jnp.where(keep, lo, zero)
        return dot(lhs, jnp.concatenate([bh, bh], axis=0)) + dot(lhs[:, :128], bl)

    for j in range(4):
        rows = slice(576 * j, 576 * j + 576)
        approx = product(lhs, lane_block == j)
        e = err_ref[0, 0, rows]
        merged = grad_ref[0, 0, rows].astype(f32) + e.astype(f32)
        en_ref[0, 0, rows] = jnp.where(live, (merged - approx).astype(bf16), e)

    fac = fac_ref[0:1, :]
    at = pl.multiple_of(lax.rem(r, 8) * 72, 8)
    rhi, rlo = split(pf_ref[pl.ds(at, 72)])
    rows_lhs = jnp.concatenate([rhi, rlo], axis=1)
    approx = product(rows_lhs, lane_block == r // 8)
    m = m_ref[0]
    mn = jnp.where(live, momentum_decay * m + fac * approx, m)
    mn_ref[0] = mn
    w = w_ref[0]
    wn_ref[0] = jnp.where(live, w - learn_rate * mn, w)
    qn_ref[0] = jnp.where(live, qt_ref[...], q_ref[0])
    vmean = vs_ref[:, :72] * (1.0 / 32.0)
    vmn = momentum_decay * vm_ref[...] + fac[:, :72] * vmean
    vmn_ref[...] = vmn
    vwn_ref[...] = vw_ref[...] - learn_rate * vmn


def on_device(owner_of, grad, error, q_prev, weight, momentum, vec_grad, vec_weight, vec_mom):
    S = jax.ShapeDtypeStruct
    vm = pl.BlockSpec(memory_space=pltpu.VMEM)
    hbm = pl.BlockSpec(memory_space=pl.ANY)
    smem = pl.BlockSpec(memory_space=pltpu.SMEM)
    width = grad.shape[2]
    entries = float(owner_of.shape[0] * width * grad.shape[3] + NO * vec_grad.shape[1] * width)
    n_sends = 3 + 7 + 7 + 3 + 3 + 7 + 3 + 3 + 7 + 7 + 7 + 3 + 7 + 15
    V = pltpu.VMEM
    q_rows = jnp.swapaxes(q_prev, 1, 2)
    pf, b, qt, vs, fac = pl.pallas_call(
        functools.partial(gather_kernel, entries=entries),
        out_shape=(S((2, 576, 128), f32), S((64, 128), f32), S((64, 128), f32), S((8, 128), f32), S((8, 128), f32)),
        in_specs=[smem, hbm, hbm, hbm, hbm],
        out_specs=(vm, vm, vm, vm, vm),
        scratch_shapes=[
            V((2, 2304, 128), bf16), V((2, 2304, 128), bf16), V((2, 32, 128), f32), V((8, 2304), bf16),
            V((2, 576, 128), f32),
            V((3, 144, 128), f32), V((8, 24, 128), f32), V((7, 24, 128), f32), V((24, 128), f32), V((8, 24, 128), f32),
            V((7, 72, 128), f32), V((4, 24, 128), f32), V((3, 24, 128), f32), V((24, 128), f32), V((4, 24, 128), f32),
            V((32, 8, 128), f32), V((3, 8, 8, 128), f32), V((8, 8, 128), f32), V((7, 8, 128), f32),
            V((8, 8, 128), f32), V((7, 8, 128), f32), V((4, 16, 128), f32), V((8, 16, 128), f32), V((16, 8, 128), f32),
            pltpu.SemaphoreType.DMA((6,)),
            pltpu.SemaphoreType.DMA((n_sends,)),
            pltpu.SemaphoreType.DMA((n_sends,)),
        ],
        compiler_params=pltpu.CompilerParams(collective_id=0, has_side_effects=True),
        name="gather",
    )(owner_of, grad, error, q_rows, vec_grad)

    full = lambda shape: pl.BlockSpec(shape, lambda s: (0,) * len(shape))
    slot = lambda shape: pl.BlockSpec((1,) + shape, lambda s: (s,) + (0,) * len(shape))
    big = pl.BlockSpec((1, 1, 2304, 128), lambda s: (0, s, 0, 0))
    half = pl.BlockSpec((32, 128), lambda s: (s, 0))
    wn, mn, en, qn, vwn, vmn = pl.pallas_call(
        update_kernel,
        grid=(2,),
        out_shape=(
            S(weight.shape, f32), S(momentum.shape, f32), S(error.shape, bf16), S(q_rows.shape, f32),
            S(vec_weight.shape, f32), S(vec_mom.shape, f32),
        ),
        in_specs=[
            smem, full((8, 128)), pl.BlockSpec((None, 576, 128), lambda s: (s, 0, 0)), half, half, full((8, 128)),
            big, big, slot((32, 128)), slot((72, 128)), slot((72, 128)), full((8, 72)), full((8, 72)),
        ],
        out_specs=(
            slot((72, 128)), slot((72, 128)), big, slot((32, 128)), full((8, 72)), full((8, 72)),
        ),
        name="update",
    )(owner_of, fac, pf, b, qt, vs, grad, error, q_rows, weight, momentum, vec_weight, vec_mom)
    return wn, mn, en, jnp.swapaxes(qn, 1, 2), vwn, vmn


def solution(mesh):
    return jax.shard_map(
        on_device,
        mesh=mesh,
        in_specs=(
            P(),
            P("replica", "owner", None, None),
            P("replica", "owner", None, None),
            P("owner", None, None),
            P("owner", "replica", None),
            P("owner", "replica", None),
            P("replica", "owner", None),
            P("owner", "replica"),
            P("owner", "replica"),
        ),
        out_specs=(
            P("owner", "replica", None),
            P("owner", "replica", None),
            P("replica", "owner", None, None),
            P("owner", None, None),
            P("owner", "replica"),
            P("owner", "replica"),
        ),
        check_vma=False,
    )
```

```python
import functools

import jax
import jax.numpy as jnp
from jax import lax
from jax.experimental import pallas as pl
from jax.experimental.pallas import tpu as pltpu
from jax.sharding import PartitionSpec as P

MESH = pl.DeviceIdType.MESH
NS_ITERS = 5
NX, NY, NO = 4, 8, 16
clip_limit = 0.1
momentum_decay = 0.9
learn_rate = 0.05
f32, bf16 = jnp.float32, jnp.bfloat16
HIGH = lax.Precision.HIGHEST
XFAR = (2, 1, 3)
YFAR = (4, 3, 5, 2, 6, 1, 7)
OFAR = (8, 7, 9, 6, 10, 5, 11, 4, 12, 3, 13, 2, 14, 1, 15)


def split(a):
    hi = a.astype(bf16)
    return hi, (a - hi.astype(f32)).astype(bf16)


def dot(a, b, dims=((1,), (0,)), precision=None):
    return lax.dot_general(a, b, (dims, ((), ())), precision=precision, preferred_element_type=f32)


def step_kernel(
    own_ref, grad_ref, err_ref, q_ref, vec_ref, w_ref, m_ref, vw_ref, vm_ref,
    wn_ref, mn_ref, en_ref, qn_ref, vwn_ref, vmn_ref,
    gv, ev, qv, vv, wv, mv, vwv, vmv, loc, pf, rx0, a0, ry0, ry1, c1, rx1, own1, gx1,
    vpk, vrx, vc, vry, vqy, vqx, tt, try_, tx, tf, sc,
    load_sem, send_sem, recv_sem,
    *, entries,
):
    r = lax.axis_index("replica")
    o = lax.axis_index("owner")
    x, y = lax.rem(r, NX), r // NX

    def xpeer(d):
        return (y * NX + lax.rem(x + d, NX), o)

    def ypeer(d):
        return (lax.rem(y + d, NY) * NX + x, o)

    def opeer(d):
        return (r, lax.rem(o + d, NO))

    barrier = pltpu.get_barrier_semaphore()
    peers = [ypeer(d) for d in YFAR] + [opeer(d) for d in OFAR] + [xpeer(d) for d in XFAR]
    for peer in peers:
        pl.semaphore_signal(barrier, inc=1, device_id=peer, device_id_type=MESH)

    loads = []
    for n, (src, dst) in enumerate(
        [(q_ref, qv), (grad_ref.at[0, 0], gv.at[0]), (err_ref.at[0, 0], ev.at[0]),
         (grad_ref.at[0, 1], gv.at[1]), (err_ref.at[0, 1], ev.at[1]), (vec_ref.at[0], vv),
         (w_ref, wv), (m_ref, mv), (vw_ref, vwv), (vm_ref, vmv)]
    ):
        copy = pltpu.make_async_copy(src, dst, load_sem.at[n])
        copy.start()
        loads.append(copy)

    started = []

    def send(src, dst, peer):
        n = len(started)
        copy = pltpu.make_async_remote_copy(
            src_ref=src, dst_ref=dst, send_sem=send_sem.at[n], recv_sem=recv_sem.at[n],
            device_id=peer, device_id_type=MESH,
        )
        copy.start()
        started.append(copy)
        return copy

    def arrive(copies):
        for copy in copies:
            copy.wait_recv()

    def rows(start, size):
        return pl.ds(pl.multiple_of(start, 8), size)

    lane_k = lax.broadcasted_iota(jnp.int32, (128, 128), 1)
    row_k = lax.broadcasted_iota(jnp.int32, (128, 128), 0)
    lane_block, row_block = lane_k // 32, row_k // 32

    def left(s):
        wide = jnp.concatenate([qv[s]] * 4, axis=0).T
        hi, lo = split(wide)
        zero = jnp.zeros_like(hi)
        total = None
        for j in range(4):
            keep = lane_block == j
            half = jnp.concatenate([jnp.where(keep, hi, zero), jnp.where(keep, lo, zero)], axis=1)
            rhs = jnp.concatenate([half, half], axis=0)
            part = slice(576 * j, 576 * j + 576)
            term = dot(jnp.concatenate([gv[s, part], ev[s, part]], axis=1), rhs)
            total = term if total is None else total + term
        loc[576 * s:576 * s + 576] = total[:, :128] + total[:, 128:]

    loads[0].wait()
    loads[3].wait()
    loads[4].wait()
    left(1)
    loads[1].wait()
    loads[2].wait()
    left(0)
    pl.semaphore_wait(barrier, len(peers))

    x0, y1 = [], []
    for n in range(7):
        to = lax.rem(y + YFAR[n], NY)
        y1.append(send(loc.at[rows(768 + to * 48, 48)], ry1.at[YFAR[n] - 1], ypeer(YFAR[n])))
        if n < 3:
            to = lax.rem(x + XFAR[n], NX)
            x0.append(send(loc.at[rows(to * 192, 192)], rx0.at[XFAR[n] - 1], xpeer(XFAR[n])))

    for load in loads[5:]:
        load.wait()
    vall = vv[...].astype(f32)
    for yy in range(NY):
        for xx in range(NX):
            at = 72 * (NX * yy + xx)
            vpk[xx * NY + yy] = jnp.concatenate([vall[:, at:at + 72], jnp.zeros((8, 56), f32)], axis=1)

    arrive(x0)
    a0[...] = loc[rows(x * 192, 192)] + rx0[0] + rx0[1] + rx0[2]
    y0 = [send(a0.at[rows(lax.rem(y + d, NY) * 24, 24)], ry0.at[d - 1], ypeer(d)) for d in YFAR]

    arrive(y1)
    acc = loc[rows(768 + y * 48, 48)]
    for d in range(7):
        acc = acc + ry1[d]
    pad4 = jnp.zeros((4, 128), f32)
    for xx in range(NX):
        c1[xx] = jnp.concatenate([acc[12 * xx:12 * xx + 12], pad4], axis=0)
    x1 = [send(c1.at[lax.rem(x + d, NX)], rx1.at[d - 1], xpeer(d)) for d in XFAR]
    vx = [send(vpk.at[pl.ds(lax.rem(x + d, NX) * NY, NY)], vrx.at[d - 1], xpeer(d)) for d in XFAR]

    arrive(x1)
    acc = c1[x] + rx1[0] + rx1[1] + rx1[2]
    own1[...] = acc
    gx1[x] = acc
    g1 = [send(own1, gx1.at[x], xpeer(d)) for d in XFAR]

    arrive(y0)
    acc = a0[rows(y * 24, 24)]
    for d in range(7):
        acc = acc + ry0[d]
    mine = rows(x * 192 + y * 24, 24)
    pf[mine] = acc
    g0 = [send(pf.at[mine], pf.at[mine], ypeer(d)) for d in YFAR]

    arrive(g1)
    block1 = rows(768 + y * 48, 48)
    pf[block1] = jnp.concatenate([gx1[xx, 0:12] for xx in range(NX)], axis=0)
    h1 = [send(pf.at[block1], pf.at[block1], ypeer(d)) for d in YFAR]

    arrive(vx)
    vc[...] = vpk[pl.ds(x * NY, NY)] + vrx[0] + vrx[1] + vrx[2]
    vy = [send(vc.at[lax.rem(y + d, NY)], vry.at[d - 1], ypeer(d)) for d in YFAR]

    arrive(g0)
    block0 = rows(x * 192, 192)
    h0 = [send(pf.at[block0], pf.at[block0], xpeer(d)) for d in XFAR]

    arrive(vy)
    vsum = vc[y]
    for d in range(7):
        vsum = vsum + vry[d]
    vmean = vsum * (1.0 / 32.0)
    vqy[y] = jnp.sum(vmean * vmean, axis=0, keepdims=True)

    def right(s):
        hi, lo = split(pf[576 * s:576 * s + 576])
        lhs = jnp.concatenate([hi, lo], axis=1)
        total = None
        for j in range(4):
            part = slice(576 * j, 576 * j + 576)
            term = dot(lhs, jnp.concatenate([gv[s, part], ev[s, part]], axis=1), ((0,), (0,)))
            term = term[32 * j:32 * j + 32] + term[128 + 32 * j:160 + 32 * j]
            total = term if total is None else total + term
        total = total[:, :128] + total[:, 128:]
        for i in range(4):
            tt[4 * s + i] = total[8 * i:8 * i + 8]

    arrive(h0)
    right(0)
    arrive(h1)
    right(1)
    ty = [send(tt.at[lax.rem(y + d, NY)], try_.at[d - 1], ypeer(d)) for d in YFAR]
    qy = [send(vqy.at[y], vqy.at[y], ypeer(d)) for d in YFAR]

    def pad(a):
        return jnp.concatenate([a, jnp.zeros((64, 128), f32)], axis=0)

    grams = []
    for s in range(2):
        p = pf[576 * s:576 * s + 576]
        wide = jnp.where(row_block == lane_block, dot(p, p, ((0,), (0,)), HIGH), 0.0)
        g = (wide[0:32] + wide[32:64]) + (wide[64:96] + wide[96:128])
        g = g + pltpu.roll(g, 64, 1)
        g = g + pltpu.roll(g, 32, 1)
        grams.append(jnp.where(lane_block[:32] == s, g, 0.0))
    gram = jnp.concatenate(grams, axis=0)
    scale = [
        jnp.sqrt(jnp.sum(jnp.sum(g * g, axis=0, keepdims=True), axis=1, keepdims=True) + 1e-06) for g in grams
    ]
    slot_of = row_k[:64, :1] // 32
    scale_row = jnp.where(slot_of == 0, scale[0], scale[1])
    eye = (row_k == lane_k).astype(f32)[:64]
    cur = gram / scale_row
    root = eye
    for step in range(NS_ITERS):
        fm = 1.5 * eye - 0.5 * (cur if step == 0 else dot(root, pad(cur), precision=HIGH))
        if step < NS_ITERS - 1:
            cur = dot(cur, pad(fm), precision=HIGH)
        root = fm if step == 0 else dot(fm, pad(root), precision=HIGH)

    arrive(ty)
    acc = tt[y]
    for d in range(7):
        acc = acc + try_[d]
    tx[x] = acc
    t2 = [send(tx.at[x], tx.at[x], xpeer(d)) for d in XFAR]
    arrive(qy)
    acc = vqy[0]
    for yy in range(1, NY):
        acc = acc + vqy[yy]
    vqx[x] = acc
    qx = [send(vqx.at[x], vqx.at[x], xpeer(d)) for d in XFAR]

    inv_sqrt = 1.0 / jnp.sqrt(scale_row)
    root_t = pad(root).T[:64]
    qm = root_t * (inv_sqrt * (1.0 / 32.0))
    bm = dot(root * inv_sqrt, pad(qm), precision=HIGH)

    arrive(t2)
    tf[y] = (tx[0] + tx[1]) + (tx[2] + tx[3])
    t3 = [send(tf.at[y], tf.at[y], ypeer(d)) for d in YFAR]

    pm = dot(root_t, pad(dot(gram, pad(root), precision=HIGH)), precision=HIGH) / scale_row
    pm = dot(pm, pad(qm), precision=HIGH)
    lhs = jnp.concatenate([qm, pm, bm], axis=0)
    arrive(qx)
    vtot = (vqx[0] + vqx[1]) + (vqx[2] + vqx[3])
    count = jnp.int32(0)
    for n in range(own_ref.shape[0]):
        count = count + jnp.where(own_ref[n] == o, 1, 0).astype(jnp.int32)
    live_row = (slot_of < count).astype(f32)

    arrive(t3)
    tfull = jnp.concatenate([tf[yy] for yy in range(NY)], axis=0)
    out = dot(lhs, pad(tfull), precision=HIGH)
    qt, pq, b = out[0:64], out[64:128], out[128:192]
    sc[o] = jnp.sum(qt * pq * live_row, axis=0, keepdims=True) + vtot
    s1 = [send(sc.at[o], sc.at[o], opeer(d)) for d in OFAR]

    approx_rows = []
    for s in range(2):
        live = s < count
        hi, lo = split(jnp.concatenate([b[32 * s:32 * s + 32]] * 4, axis=0))
        zero = jnp.zeros_like(hi)

        def product(p, keep):
            phi, plo = split(p)
            bh, bl = jnp.where(keep, hi, zero), jnp.where(keep, lo, zero)
            return dot(jnp.concatenate([phi, plo], axis=1), jnp.concatenate([bh, bh], axis=0)) + dot(phi, bl)

        for j in range(4):
            part = slice(576 * j, 576 * j + 576)
            approx = product(pf[576 * s:576 * s + 576], row_block == j)
            e = ev[s, part]
            merged = gv[s, part].astype(f32) + e.astype(f32)
            en_ref[0, s, part] = jnp.where(live, (merged - approx).astype(bf16), e)
        approx_rows.append(product(pf[rows(576 * s + lax.rem(r, 8) * 72, 72)], row_block == r // 8))
        qn_ref[s] = jnp.where(live, qt[32 * s:32 * s + 32], qv[s])

    arrive(s1)
    total = sc[0]
    for n in range(1, NO):
        total = total + sc[n]
    total_sq = jnp.sum(total, axis=1, keepdims=True)
    fac = jnp.minimum(1.0, clip_limit / jnp.sqrt(total_sq / entries + 1e-06))
    for s in range(2):
        live = s < count
        m = mv[s]
        mn = jnp.where(live, momentum_decay * m + fac * approx_rows[s], m)
        mn_ref[s] = mn
        wn_ref[s] = jnp.where(live, wv[s] - learn_rate * mn, wv[s])
    vmn = momentum_decay * vmv[...] + fac * vmean[:, :72]
    vmn_ref[...] = vmn
    vwn_ref[...] = vwv[...] - learn_rate * vmn
    for copy in started:
        copy.wait_send()


def move_kernel(*refs):
    n = len(refs) // 2
    copies = [pltpu.make_async_copy(refs[i], refs[n + i], refs[2 * n].at[i]) for i in (2, 0, 1, 3, 4, 5)]
    for copy in copies:
        copy.start()
    for copy in copies:
        copy.wait()


def on_device(owner_of, grad, error, q_prev, weight, momentum, vec_grad, vec_weight, vec_mom):
    S = jax.ShapeDtypeStruct
    vm = pl.BlockSpec(memory_space=pltpu.VMEM)
    hbm = pl.BlockSpec(memory_space=pltpu.HBM)
    smem = pl.BlockSpec(memory_space=pltpu.SMEM)
    width = grad.shape[2]
    entries = float(owner_of.shape[0] * width * grad.shape[3] + NO * vec_grad.shape[1] * width)
    n_sends = 3 + 7 + 7 + 3 + 3 + 3 + 7 + 7 + 7 + 3 + 7 + 7 + 3 + 3 + 7 + 15
    V = pltpu.VMEM
    q_rows = jnp.swapaxes(q_prev, 1, 2)
    shapes = (
        S(weight.shape, f32), S(momentum.shape, f32), S(error.shape, bf16), S(q_rows.shape, f32),
        S(vec_weight.shape, f32), S(vec_mom.shape, f32),
    )
    results = pl.pallas_call(
        functools.partial(step_kernel, entries=entries),
        out_shape=shapes,
        in_specs=[smem] + [hbm] * 8,
        out_specs=(vm,) * 6,
        scratch_shapes=[
            V((2, 2304, 128), bf16), V((2, 2304, 128), bf16), V((2, 32, 128), f32), V((8, 2304), bf16),
            V((2, 72, 128), f32), V((2, 72, 128), f32), V((8, 72), f32), V((8, 72), f32),
            V((1152, 128), f32), V((1152, 128), f32),
            V((3, 192, 128), f32), V((192, 128), f32), V((7, 24, 128), f32),
            V((7, 48, 128), f32), V((4, 16, 128), f32), V((3, 16, 128), f32), V((16, 128), f32), V((4, 16, 128), f32),
            V((32, 8, 128), f32), V((3, 8, 8, 128), f32), V((8, 8, 128), f32), V((7, 8, 128), f32),
            V((8, 1, 128), f32), V((4, 1, 128), f32),
            V((8, 8, 128), f32), V((7, 8, 128), f32), V((4, 8, 128), f32), V((8, 8, 128), f32), V((16, 1, 128), f32),
            pltpu.SemaphoreType.DMA((10,)),
            pltpu.SemaphoreType.DMA((n_sends,)),
            pltpu.SemaphoreType.DMA((n_sends,)),
        ],
        compiler_params=pltpu.CompilerParams(collective_id=0, has_side_effects=True, vmem_limit_bytes=24 << 20),
        name="step",
    )(owner_of, grad, error, q_rows, vec_grad, weight, momentum, vec_weight, vec_mom)
    wn, mn, en, qn, vwn, vmn = pl.pallas_call(
        move_kernel,
        out_shape=shapes,
        in_specs=[vm] * 6,
        out_specs=(hbm,) * 6,
        scratch_shapes=[pltpu.SemaphoreType.DMA((6,))],
        compiler_params=pltpu.CompilerParams(vmem_limit_bytes=8 << 20),
        name="move",
    )(*results)
    return wn, mn, en, jnp.swapaxes(qn, 1, 2), vwn, vmn


def solution(mesh):
    return jax.shard_map(
        on_device,
        mesh=mesh,
        in_specs=(
            P(),
            P("replica", "owner", None, None),
            P("replica", "owner", None, None),
            P("owner", None, None),
            P("owner", "replica", None),
            P("owner", "replica", None),
            P("replica", "owner", None),
            P("owner", "replica"),
            P("owner", "replica"),
        ),
        out_specs=(
            P("owner", "replica", None),
            P("owner", "replica", None),
            P("replica", "owner", None, None),
            P("owner", None, None),
            P("owner", "replica"),
            P("owner", "replica"),
        ),
        check_vma=False,
    )
```

```python
import functools

import jax
import jax.numpy as jnp
from jax import lax
from jax.experimental import pallas as pl
from jax.experimental.pallas import tpu as pltpu
from jax.sharding import PartitionSpec as P

MESH = pl.DeviceIdType.MESH
NS_ITERS = 5
NX, NY, NO = 4, 8, 16
clip_limit = 0.1
momentum_decay = 0.9
learn_rate = 0.05
f32, bf16 = jnp.float32, jnp.bfloat16
HIGH = lax.Precision.HIGHEST
XFAR = (2, 1, 3)
YFAR = (4, 3, 5, 2, 6, 1, 7)
YNEAR = (1, 7, 2, 6, 3, 5, 4)
OFAR = (8, 7, 9, 6, 10, 5, 11, 4, 12, 3, 13, 2, 14, 1, 15)


def split(a):
    hi = a.astype(bf16)
    return hi, (a - hi.astype(f32)).astype(bf16)


def dot(a, b, dims=((1,), (0,)), precision=None):
    return lax.dot_general(a, b, (dims, ((), ())), precision=precision, preferred_element_type=f32)


def step_kernel(
    own_ref, grad_ref, err_ref, q_ref, vec_ref, w_ref, m_ref, vw_ref, vm_ref,
    wn_ref, mn_ref, en_ref, qn_ref, vwn_ref, vmn_ref,
    gv, ev, qv, vv, wv, mv, vwv, vmv, loc, pf, pc, rx0, a0, ry0,
    vpk, vrx, vc, vry, vqy, vqx, tt, try_, tx, tf, sc, env,
    load_sem, send_sem, recv_sem,
    *, entries,
):
    r = lax.axis_index("replica")
    o = lax.axis_index("owner")
    x, y = lax.rem(r, NX), r // NX

    def xpeer(d):
        return (y * NX + lax.rem(x + d, NX), o)

    def ypeer(d):
        return (lax.rem(y + d, NY) * NX + x, o)

    def opeer(d):
        return (r, lax.rem(o + d, NO))

    barrier = pltpu.get_barrier_semaphore()
    peers = [ypeer(d) for d in YFAR] + [opeer(d) for d in OFAR] + [xpeer(d) for d in XFAR]
    for peer in peers:
        pl.semaphore_signal(barrier, inc=1, device_id=peer, device_id_type=MESH)

    loads = []
    for n, (src, dst) in enumerate(
        [(q_ref, qv), (grad_ref.at[0, 0], gv.at[0]), (err_ref.at[0, 0], ev.at[0]),
         (grad_ref.at[0, 1], gv.at[1]), (err_ref.at[0, 1], ev.at[1]), (vec_ref.at[0], vv),
         (w_ref, wv), (m_ref, mv), (vw_ref, vwv), (vm_ref, vmv)]
    ):
        copy = pltpu.make_async_copy(src, dst, load_sem.at[n])
        copy.start()
        loads.append(copy)

    started = []

    def send(src, dst, peer):
        n = len(started)
        copy = pltpu.make_async_remote_copy(
            src_ref=src, dst_ref=dst, send_sem=send_sem.at[n], recv_sem=recv_sem.at[n],
            device_id=peer, device_id_type=MESH,
        )
        copy.start()
        started.append(copy)
        return copy

    def arrive(copies):
        for copy in copies:
            copy.wait_recv()

    def rows(start, size):
        return pl.ds(pl.multiple_of(start, 8), size)

    lane_k = lax.broadcasted_iota(jnp.int32, (128, 128), 1)
    row_k = lax.broadcasted_iota(jnp.int32, (128, 128), 0)
    lane_block, row_block = lane_k // 32, row_k // 32

    def left(s):
        wide = jnp.concatenate([qv[s]] * 4, axis=0).T
        hi, lo = split(wide)
        zero = jnp.zeros_like(hi)
        total = None
        for j in range(4):
            keep = lane_block == j
            half = jnp.concatenate([jnp.where(keep, hi, zero), jnp.where(keep, lo, zero)], axis=1)
            rhs = jnp.concatenate([half, half], axis=0)
            part = slice(576 * j, 576 * j + 576)
            term = dot(jnp.concatenate([gv[s, part], ev[s, part]], axis=1), rhs)
            total = term if total is None else total + term
        total = total[:, :128] + total[:, 128:]
        for i in range(16):
            loc[16 * s + i] = total[36 * i:36 * i + 36]

    loads[0].wait()
    loads[3].wait()
    loads[4].wait()
    left(1)
    loads[1].wait()
    loads[2].wait()
    left(0)
    pl.semaphore_wait(barrier, len(peers))

    x0 = []
    for k, e in enumerate(YFAR + (0,)):
        to_y = lax.rem(y + e, NY)
        x0.append([send(loc.at[lax.rem(x + d, NX) * NY + to_y], rx0.at[d - 1, k], xpeer(d)) for d in XFAR])

    for load in loads[5:]:
        load.wait()
    vall = vv[...].astype(f32)
    for yy in range(NY):
        for xx in range(NX):
            at = 72 * (NX * yy + xx)
            vpk[xx * NY + yy] = jnp.concatenate([vall[:, at:at + 72], jnp.zeros((8, 56), f32)], axis=1)

    y0 = []
    for k, e in enumerate(YFAR + (0,)):
        arrive(x0[k])
        acc = (loc[x * NY + lax.rem(y + e, NY)] + rx0[0, k]) + (rx0[1, k] + rx0[2, k])
        if e:
            a0[k] = acc
            y0.append(send(a0.at[k], ry0.at[e - 1], ypeer(e)))
    vx = [send(vpk.at[pl.ds(lax.rem(x + d, NX) * NY, NY)], vrx.at[d - 1], xpeer(d)) for d in XFAR]

    arrive(y0)
    for d in range(7):
        acc = acc + ry0[d]
    mine = x * NY + y
    pf[mine] = acc
    g0 = {e: send(pf.at[mine], pf.at[mine], ypeer(e)) for e in YFAR}
    h0 = [send(pf.at[mine], pf.at[mine], xpeer(d)) for d in XFAR]
    for e in YNEAR:
        arrive([g0[e]])
        block = x * NY + lax.rem(y + NY - e, NY)
        h0 += [send(pf.at[block], pf.at[block], xpeer(d)) for d in XFAR]

    arrive(vx)
    vc[...] = vpk[pl.ds(x * NY, NY)] + vrx[0] + vrx[1] + vrx[2]
    vy = [send(vc.at[lax.rem(y + d, NY)], vry.at[d - 1], ypeer(d)) for d in YFAR]

    arrive(vy)
    vsum = vc[y]
    for d in range(7):
        vsum = vsum + vry[d]
    vmean = vsum * (1.0 / 32.0)
    vqy[y] = jnp.sum(vmean * vmean, axis=0, keepdims=True)

    def right(s):
        p = jnp.concatenate([pf[16 * s + i] for i in range(16)], axis=0)
        pc[576 * s:576 * s + 576] = p
        hi, lo = split(p)
        lhs = jnp.concatenate([hi, lo], axis=1)
        total = None
        for j in range(4):
            part = slice(576 * j, 576 * j + 576)
            term = dot(lhs, jnp.concatenate([gv[s, part], ev[s, part]], axis=1), ((0,), (0,)))
            term = term[32 * j:32 * j + 32] + term[128 + 32 * j:160 + 32 * j]
            total = term if total is None else total + term
        total = total[:, :128] + total[:, 128:]
        for i in range(4):
            tt[4 * s + i] = total[8 * i:8 * i + 8]

    arrive(h0)
    right(0)
    right(1)
    ty = [send(tt.at[lax.rem(y + d, NY)], try_.at[d - 1], ypeer(d)) for d in YFAR]
    qy = [send(vqy.at[y], vqy.at[y], ypeer(d)) for d in YFAR]

    def pad(a):
        return jnp.concatenate([a, jnp.zeros((64, 128), f32)], axis=0)

    grams = []
    for s in range(2):
        p = pc[576 * s:576 * s + 576]
        wide = jnp.where(row_block == lane_block, dot(p, p, ((0,), (0,)), HIGH), 0.0)
        g = (wide[0:32] + wide[32:64]) + (wide[64:96] + wide[96:128])
        g = g + pltpu.roll(g, 64, 1)
        g = g + pltpu.roll(g, 32, 1)
        grams.append(jnp.where(lane_block[:32] == s, g, 0.0))
    gram = jnp.concatenate(grams, axis=0)
    scale = [
        jnp.sqrt(jnp.sum(jnp.sum(g * g, axis=0, keepdims=True), axis=1, keepdims=True) + 1e-06) for g in grams
    ]
    slot_of = row_k[:64, :1] // 32
    scale_row = jnp.where(slot_of == 0, scale[0], scale[1])
    eye = (row_k == lane_k).astype(f32)[:64]
    cur = gram / scale_row
    root = eye
    for step in range(NS_ITERS):
        fm = 1.5 * eye - 0.5 * (cur if step == 0 else dot(root, pad(cur), precision=HIGH))
        if step < NS_ITERS - 1:
            cur = dot(cur, pad(fm), precision=HIGH)
        root = fm if step == 0 else dot(fm, pad(root), precision=HIGH)

    arrive(ty)
    acc = tt[y]
    for d in range(7):
        acc = acc + try_[d]
    tx[x] = acc
    t2 = [send(tx.at[x], tx.at[x], xpeer(d)) for d in XFAR]
    arrive(qy)
    acc = vqy[0]
    for yy in range(1, NY):
        acc = acc + vqy[yy]
    vqx[x] = acc
    qx = [send(vqx.at[x], vqx.at[x], xpeer(d)) for d in XFAR]

    inv_sqrt = 1.0 / jnp.sqrt(scale_row)
    root_t = pad(root).T[:64]
    qm = root_t * (inv_sqrt * (1.0 / 32.0))
    bm = dot(root * inv_sqrt, pad(qm), precision=HIGH)

    arrive(t2)
    tf[y] = (tx[0] + tx[1]) + (tx[2] + tx[3])
    t3 = [send(tf.at[y], tf.at[y], ypeer(d)) for d in YFAR]

    pm = dot(root_t, pad(dot(gram, pad(root), precision=HIGH)), precision=HIGH) / scale_row
    pm = dot(pm, pad(qm), precision=HIGH)
    lhs = jnp.concatenate([qm, pm, bm], axis=0)
    arrive(qx)
    vtot = (vqx[0] + vqx[1]) + (vqx[2] + vqx[3])
    count = jnp.int32(0)
    for n in range(own_ref.shape[0]):
        count = count + jnp.where(own_ref[n] == o, 1, 0).astype(jnp.int32)
    live_row = (slot_of < count).astype(f32)

    arrive(t3)
    tfull = jnp.concatenate([tf[yy] for yy in range(NY)], axis=0)
    out = dot(lhs, pad(tfull), precision=HIGH)
    qt, pq, b = out[0:64], out[64:128], out[128:192]
    sc[o] = jnp.sum(qt * pq * live_row, axis=0, keepdims=True) + vtot
    s1 = [send(sc.at[o], sc.at[o], opeer(d)) for d in OFAR]

    approx_rows, puts = [], []
    for s in range(2):
        live = s < count
        hi, lo = split(jnp.concatenate([b[32 * s:32 * s + 32]] * 4, axis=0))
        zero = jnp.zeros_like(hi)

        def product(p, keep):
            phi, plo = split(p)
            bh, bl = jnp.where(keep, hi, zero), jnp.where(keep, lo, zero)
            return dot(jnp.concatenate([phi, plo], axis=1), jnp.concatenate([bh, bh], axis=0)) + dot(phi, bl)

        for j in range(4):
            part = slice(576 * j, 576 * j + 576)
            approx = product(pc[576 * s:576 * s + 576], row_block == j)
            e = ev[s, part]
            merged = gv[s, part].astype(f32) + e.astype(f32)
            env[s, part] = jnp.where(live, (merged - approx).astype(bf16), e)
        approx_rows.append(product(pc[rows(576 * s + lax.rem(r, 8) * 72, 72)], row_block == r // 8))
        put = pltpu.make_async_copy(env.at[s], en_ref.at[0, s], load_sem.at[10 + s])
        put.start()
        puts.append(put)
        qn_ref[s] = jnp.where(live, qt[32 * s:32 * s + 32], qv[s])

    arrive(s1)
    total = sc[0]
    for n in range(1, NO):
        total = total + sc[n]
    total_sq = jnp.sum(total, axis=1, keepdims=True)
    fac = jnp.minimum(1.0, clip_limit / jnp.sqrt(total_sq / entries + 1e-06))
    for s in range(2):
        live = s < count
        m = mv[s]
        mn = jnp.where(live, momentum_decay * m + fac * approx_rows[s], m)
        mn_ref[s] = mn
        wn_ref[s] = jnp.where(live, wv[s] - learn_rate * mn, wv[s])
    vmn = momentum_decay * vmv[...] + fac * vmean[:, :72]
    vmn_ref[...] = vmn
    vwn_ref[...] = vwv[...] - learn_rate * vmn
    for put in puts:
        put.wait()
    for copy in started:
        copy.wait_send()


def move_kernel(*refs):
    src, dst, held = refs[0:6], refs[6:12], refs[12:18]
    in_sem, out_sem = refs[18:]
    parts = [(2, (0, i, pl.ds(1152 * h, 1152))) for i in range(2) for h in range(2)]
    parts += [(i, (Ellipsis,)) for i in (0, 1, 3, 4, 5)]
    loads, puts = [], []
    for n, (i, at) in enumerate(parts):
        loads.append(pltpu.make_async_copy(src[i].at[at], held[i].at[at], in_sem.at[n]))
        puts.append(pltpu.make_async_copy(held[i].at[at], dst[i].at[at], out_sem.at[n]))
        loads[-1].start()
    for load, put in zip(loads, puts):
        load.wait()
        put.start()
    for put in puts:
        put.wait()


def on_device(owner_of, grad, error, q_prev, weight, momentum, vec_grad, vec_weight, vec_mom):
    S = jax.ShapeDtypeStruct
    vm = pl.BlockSpec(memory_space=pltpu.VMEM)
    hbm = pl.BlockSpec(memory_space=pltpu.HBM)
    smem = pl.BlockSpec(memory_space=pltpu.SMEM)
    width = grad.shape[2]
    entries = float(owner_of.shape[0] * width * grad.shape[3] + NO * vec_grad.shape[1] * width)
    n_sends = 24 + 7 + 3 + 7 + 24 + 7 + 7 + 7 + 3 + 3 + 7 + 15
    V = pltpu.VMEM
    q_rows = jnp.swapaxes(q_prev, 1, 2)
    shapes = (
        S(weight.shape, f32), S(momentum.shape, f32), S(error.shape, bf16), S(q_rows.shape, f32),
        S(vec_weight.shape, f32), S(vec_mom.shape, f32),
    )
    results = pl.pallas_call(
        functools.partial(step_kernel, entries=entries),
        out_shape=shapes,
        in_specs=[smem] + [hbm] * 8,
        out_specs=(vm, vm, hbm, vm, vm, vm),
        scratch_shapes=[
            V((2, 2304, 128), bf16), V((2, 2304, 128), bf16), V((2, 32, 128), f32), V((8, 2304), bf16),
            V((2, 72, 128), f32), V((2, 72, 128), f32), V((8, 72), f32), V((8, 72), f32),
            V((32, 36, 128), f32), V((32, 36, 128), f32), V((1152, 128), f32),
            V((3, 8, 36, 128), f32), V((7, 36, 128), f32), V((7, 36, 128), f32),
            V((32, 8, 128), f32), V((3, 8, 8, 128), f32), V((8, 8, 128), f32), V((7, 8, 128), f32),
            V((8, 1, 128), f32), V((4, 1, 128), f32),
            V((8, 8, 128), f32), V((7, 8, 128), f32), V((4, 8, 128), f32), V((8, 8, 128), f32), V((16, 1, 128), f32),
            V((2, 2304, 128), bf16),
            pltpu.SemaphoreType.DMA((12,)),
            pltpu.SemaphoreType.DMA((n_sends,)),
            pltpu.SemaphoreType.DMA((n_sends,)),
        ],
        compiler_params=pltpu.CompilerParams(collective_id=0, has_side_effects=True),
        name="step",
    )(owner_of, grad, error, q_rows, vec_grad, weight, momentum, vec_weight, vec_mom)
    wn, mn, en, qn, vwn, vmn = pl.pallas_call(
        move_kernel,
        out_shape=shapes,
        in_specs=[hbm] * 6,
        out_specs=(hbm,) * 6,
        scratch_shapes=[V(t.shape, t.dtype) for t in shapes] + [pltpu.SemaphoreType.DMA((9,))] * 2,
        name="move",
    )(*results)
    return wn, mn, en, jnp.swapaxes(qn, 1, 2), vwn, vmn


def solution(mesh):
    return jax.shard_map(
        on_device,
        mesh=mesh,
        in_specs=(
            P(),
            P("replica", "owner", None, None),
            P("replica", "owner", None, None),
            P("owner", None, None),
            P("owner", "replica", None),
            P("owner", "replica", None),
            P("replica", "owner", None),
            P("owner", "replica"),
            P("owner", "replica"),
        ),
        out_specs=(
            P("owner", "replica", None),
            P("owner", "replica", None),
            P("replica", "owner", None, None),
            P("owner", None, None),
            P("owner", "replica"),
            P("owner", "replica"),
        ),
        check_vma=False,
    )
```
